32 devices in a mesh: groups: 2 (over y), seq: 4 (over z), tp: 2 (over x), kv: 2 (over core).
Axes of the slice: x: 2, y: 2, z: 4, core: 2. Of those that a mesh axis runs over, the one named last changes fastest.
Arguments:
- events: bfloat16 [8, 512, 2048], P('groups', 'seq', ('tp', 'kv')), parts along dimension 0, may hold values from -6 to 6
- history_cache: bfloat16 [2, 8, 512, 1024], P(None, ('groups', 'seq'), None, ('tp', 'kv')), parts along dimension 1, may hold values from -6 to 6
- block_counts: int32 [8], P(('groups', 'seq')), parts along dimension 0, may hold values from 1 to 4
- semantic_ids: int32 [4, 128], P(None, ('groups', 'seq')), parts along dimension 1, may hold values from 0 to 4095
- beam_parents: int32 [3, 128], P(None, ('groups', 'seq')), parts along dimension 1, may hold values from 0 to 15
- query_weight: bfloat16 [2048, 2048], P('seq', ('tp', 'kv')), may hold values from -0.125 to 0.125
- keyval_weight: bfloat16 [2, 2048, 1024], P(None, 'seq', ('tp', 'kv')), may hold values from -0.125 to 0.125
- out_weight: bfloat16 [2048, 2048], P('seq', ('tp', 'kv')), may hold values from -0.125 to 0.125
- cross_weight: bfloat16 [2, 2048, 1024], P(None, 'seq', ('tp', 'kv')), may hold values from -0.125 to 0.125
- decoder_query: bfloat16 [2048, 2048], P(None, ('tp', 'kv')), may hold values from -0.125 to 0.125
- decoder_out: bfloat16 [2048, 2048], P(None, ('tp', 'kv')), may hold values from -0.125 to 0.125
- code_table: bfloat16 [4096, 2048], P(('tp', 'kv')), may hold values from -6 to 6
- encoder_gain: float32 [2048], replicated, may hold values from 0.25 to 1.75
- cross_gain: float32 [2048], replicated, may hold values from 0.25 to 1.75
- decoder_gain: float32 [2048], replicated, may hold values from 0.25 to 1.75
Outputs:
- encoded: bfloat16 [8, 512, 2048], P(('groups', 'seq'), ('tp', 'kv')), parts along dimension 0
- beam_state: bfloat16 [128, 2048], P(('groups', 'seq'), ('tp', 'kv')), parts along dimension 0
The draws below stay inside these ranges and needn't reach their ends.
There are 2 independent parts, one for each index of `groups`. The reference program is written for one: setup_inputs(seed, part) draws one part's arguments, and reference() takes and returns one part's arrays. A program takes and returns all parts, laid end to end along the dimension named above; an argument that names none is the same for every part. Nothing has to cross between parts.
Inputs may be any that keep to these rules, and one draw needn't show every extreme that they name: A user's first 128 * block_counts new events are real; the rest are padding. `semantic_ids`: the codebook entry decoded for each beam row. `beam_parents`: the beam of the previous step that each beam row continues, counted among its user's 16 beams.
All inputs are finite; a program needn't handle non-finite values.
Results may differ from the reference program's by a relative error of at most 0.014.
Values may be sent and summed in bfloat16 or wider, within the bound.
A program may use at most 64 MiB of HBM per device.

```python
import jax
import jax.numpy as jnp
from jax import lax

D = 2048
H = 16
DH = 128
KVH = 8
V = 4096
EV = 512
BLK = 128
HIST = 512
BEAMS = 16
STEPS = 4
USERS = 4
N_TP = 2
N_KV = 2


def touch_ends(array, stream_key, low, largest):
    longest = array.shape.index(max(array.shape))
    spots = []
    for shift in (0, 1):
        where = [jax.random.randint(jax.random.fold_in(stream_key, axis), (), 0, length) for axis, length in enumerate(array.shape)]
        where[longest] = (where[longest] + shift) % array.shape[longest]
        spots.append(tuple(where))
    return array.at[spots[0]].set(low).at[spots[1]].set(largest)


def levels(rng, dims, cuts, smallest, top_value):
    gain, own = 1.0, jax.random.fold_in(rng, 6)
    for dim, blocks in cuts:
        heights = jnp.exp(jax.random.uniform(jax.random.fold_in(own, dim), (blocks,), jnp.float32, smallest / len(cuts), top_value / len(cuts)))
        gain = gain * jnp.repeat(heights, dims[dim] // blocks).reshape([-1 if axis == dim else 1 for axis in range(len(dims))])
    return gain


def scatter_about(rng, dims, scale, limit, split=(), held_as=jnp.bfloat16):
    values = jax.random.normal(rng, dims, jnp.float32) * scale
    if len(split) > 0:
        values = levels(rng, dims, split, -0.22, 0.18) * values
    return jnp.clip(values, min=-limit, max=limit).astype(held_as)


def setup_inputs(seed: int = 0, part: int = 0) -> dict:
    keys = jax.random.split(jax.random.key(seed), 16)
    part_keys = jax.random.split(jax.random.fold_in(keys[15], part), 16)
    return {
        "events": scatter_about(part_keys[0], (USERS, EV, D), 1.0, 6.0, ((1, 4), (2, 4))),
        "history_cache": scatter_about(part_keys[1], (2, USERS, HIST, KVH * DH), 1.0, 6.0, ((1, 4), (3, 4))),
        "block_counts": touch_ends(jax.random.randint(part_keys[2], (USERS,), 1, EV // BLK + 1), jax.random.fold_in(part_keys[2], 1), 1, (EV // BLK + 1) - 1).astype(jnp.int32),
        "semantic_ids": touch_ends(jax.random.randint(part_keys[3], (STEPS, USERS * BEAMS), 0, V), jax.random.fold_in(part_keys[3], 1), 0, V - 1).astype(jnp.int32),
        "beam_parents": touch_ends(jax.random.randint(part_keys[4], (STEPS - 1, USERS * BEAMS), 0, BEAMS), jax.random.fold_in(part_keys[4], 1), 0, BEAMS - 1).astype(jnp.int32),
        "query_weight": scatter_about(keys[5], (D, H * DH), D ** -0.5, 0.125, ((0, 4), (1, 4))),
        "keyval_weight": scatter_about(keys[6], (2, D, KVH * DH), D ** -0.5, 0.125, ((1, 4), (2, 4))),
        "out_weight": scatter_about(keys[7], (D, H * DH), (H * DH) ** -0.5, 0.125, ((0, 4), (1, 4))),
        "cross_weight": scatter_about(keys[8], (2, D, KVH * DH), D ** -0.5, 0.125, ((1, 4), (2, 4))),
        "decoder_query": scatter_about(keys[9], (D, H * DH), D ** -0.5, 0.125, ((1, 4),)),
        "decoder_out": scatter_about(keys[10], (D, H * DH), (H * DH) ** -0.5, 0.125, ((1, 4),)),
        "code_table": scatter_about(keys[11], (V, D), 1.0, 6.0, ((0, 4),)),
        "encoder_gain": jnp.clip(1.0 + 0.15 * jax.random.normal(keys[12], (D,), jnp.float32), 0.25, 1.75),
        "cross_gain": jnp.clip(1.0 + 0.15 * jax.random.normal(keys[13], (D,), jnp.float32), 0.25, 1.75),
        "decoder_gain": jnp.clip(1.0 + 0.15 * jax.random.normal(keys[14], (D,), jnp.float32), 0.25, 1.75),
    }


eps = 1e-06

def root_norm(values, scale_gain):
    mean_square = lax.optimization_barrier(jnp.mean(values * values, axis=-1, keepdims=True))
    return values * lax.rsqrt(mean_square + eps) * scale_gain.astype(jnp.float32)

def encode_user(item, query_weight, keyval_weight, out_weight, cross_weight, encoder_gain, cross_gain):
    user_events, user_cache, user_blocks = item
    groups = N_TP * N_KV
    per_group = H // groups
    group_ratio = H // KVH
    source = user_events.astype(jnp.float32)
    normed = root_norm(source, encoder_gain).astype(jnp.bfloat16)
    queries = jnp.dot(normed, query_weight, preferred_element_type=jnp.float32).astype(jnp.bfloat16)
    keys_new = jnp.dot(normed, keyval_weight[0], preferred_element_type=jnp.float32).astype(jnp.bfloat16)
    values_new = jnp.dot(normed, keyval_weight[1], preferred_element_type=jnp.float32).astype(jnp.bfloat16)
    keys_all = jnp.concatenate([user_cache[0], keys_new], axis=0)
    values_all = jnp.concatenate([user_cache[1], values_new], axis=0)
    query_heads = queries.reshape(EV, KVH, group_ratio, DH).astype(jnp.float32)
    key_heads = keys_all.reshape(HIST + EV, KVH, DH).astype(jnp.float32)
    value_heads = values_all.reshape(HIST + EV, KVH, DH).astype(jnp.float32)
    scores = jnp.einsum('igad,jgd->gaij', query_heads, key_heads) * DH ** (-0.5)
    query_index = jnp.arange(EV, dtype=jnp.int32)[:, None]
    key_index = jnp.arange(HIST + EV, dtype=jnp.int32)[None, :] - HIST
    visible = (key_index < 0) | (key_index <= query_index) & (key_index < user_blocks * BLK)
    raised = jnp.where(visible, jnp.exp(scores), jnp.float32(0.0))
    denominator = lax.optimization_barrier(jnp.sum(raised, axis=-1, keepdims=True))
    softened = (raised / denominator).astype(jnp.bfloat16)
    attended = jnp.einsum('gaij,jgd->igad', softened.astype(jnp.float32), value_heads)
    attended = attended.reshape(EV, H * DH).astype(jnp.bfloat16)
    grouped = attended.reshape(EV, groups, per_group * DH).astype(jnp.float32)
    out_grouped = out_weight.reshape(D, groups, per_group * DH).astype(jnp.float32)
    group_terms = jnp.einsum('igc,ogc->gio', grouped, out_grouped).astype(jnp.bfloat16)
    encoded_full = source + lax.optimization_barrier(jnp.sum(group_terms.astype(jnp.float32), axis=0))
    cross_in = root_norm(encoded_full, cross_gain).astype(jnp.bfloat16)
    cross_keys = jnp.dot(cross_in, cross_weight[0], preferred_element_type=jnp.float32).astype(jnp.bfloat16)
    cross_values = jnp.dot(cross_in, cross_weight[1], preferred_element_type=jnp.float32).astype(jnp.bfloat16)
    return (encoded_full.astype(jnp.bfloat16), cross_keys, cross_values)

def reference(events, history_cache, block_counts, semantic_ids, beam_parents, query_weight, keyval_weight, out_weight, cross_weight, decoder_query, decoder_out, code_table, encoder_gain, cross_gain, decoder_gain):
    cache_users = jnp.moveaxis(history_cache, 1, 0)
    encoded, cross_keys, cross_values = lax.map(lambda item: encode_user(item, query_weight, keyval_weight, out_weight, cross_weight, encoder_gain, cross_gain), (events, cache_users, block_counts))
    group_ratio = H // KVH
    key_heads = cross_keys.reshape(USERS, EV, KVH, DH).astype(jnp.float32)
    value_heads = cross_values.reshape(USERS, EV, KVH, DH).astype(jnp.float32)
    live_events = jnp.arange(EV, dtype=jnp.int32)[None, :] < (block_counts * BLK)[:, None]
    live_mask = live_events[:, None, None, None, :]

    def attend(beam_hidden):
        normed = root_norm(beam_hidden, decoder_gain).astype(jnp.bfloat16)
        beam_queries = jnp.dot(normed, decoder_query, preferred_element_type=jnp.float32).astype(jnp.bfloat16)
        query_heads = beam_queries.reshape(USERS, BEAMS, KVH, group_ratio, DH).astype(jnp.float32)
        beam_scores = jnp.einsum('ubgad,ujgd->ugabj', query_heads, key_heads) * DH ** (-0.5)
        raised = jnp.where(live_mask, jnp.exp(beam_scores), jnp.float32(0.0))
        denominator = lax.optimization_barrier(jnp.sum(raised, axis=-1, keepdims=True))
        softened = (raised / denominator).astype(jnp.bfloat16)
        attended = jnp.einsum('ugabj,ujgd->ubgad', softened.astype(jnp.float32), value_heads)
        attended = attended.reshape(USERS * BEAMS, H * DH).astype(jnp.bfloat16)
        return lax.dot_general(attended, decoder_out, (((1,), (1,)), ((), ())), preferred_element_type=jnp.float32)
    code_rows = code_table.astype(jnp.float32)
    all_rows = jnp.arange(USERS * BEAMS, dtype=jnp.int32)
    beam_hidden = jnp.take(code_rows, semantic_ids[0], axis=0)
    mixed_state = attend(beam_hidden)
    for level in range(1, STEPS):
        source_rows = all_rows // BEAMS * BEAMS + beam_parents[level - 1]
        beam_hidden = jnp.take(beam_hidden + mixed_state, source_rows, axis=0) + jnp.take(code_rows, semantic_ids[level], axis=0)
        mixed_state = attend(beam_hidden)
    return (encoded, (beam_hidden + mixed_state).astype(jnp.bfloat16))
```

```python
import functools

import jax
import jax.numpy as jnp
from jax import lax
from jax.experimental import pallas as pl
from jax.experimental.pallas import tpu as pltpu
from jax.sharding import PartitionSpec as P

DH = 128
BLK = 128
eps = 1e-06
F32 = jnp.float32
BF16 = jnp.bfloat16
MESH = pl.DeviceIdType.MESH


def unit(values):
    return lax.rsqrt(jnp.mean(values * values, axis=-1, keepdims=True) + eps)


def dot(a, b):
    return jnp.dot(a, b, preferred_element_type=F32)


def dot_t(a, b):
    return lax.dot_general(a, b, (((1,), (1,)), ((), ())), preferred_element_type=F32)


def body(
    sizes,
    events, history, counts, ids, parents, wq_in, wkv_in, wo_in, wc_in, dq_in, do_in, table_in,
    egain, cgain, dgain,
    enc_out, beam_out,
    wq, wkv, wo, wc, dq, do, table, hist, xb, normed, qs, kn, vn, att, gterm, rk, s1, rt, cx, ck, cv,
    look, terms, last_own, last_in, hidden_ref, mixed_ref, ba,
    local_sem, z_send, z_recv, y_send, y_recv, ev_send, ev_recv,
    ag_send, ag_recv, lk_send, lk_recv, rk_send, rk_recv, rt_send, rt_recv, tm_send, tm_recv,
):
    G, S, T, K = sizes
    TK = T * K
    g, s = lax.axis_index("groups"), lax.axis_index("seq")
    t, k = lax.axis_index("tp"), lax.axis_index("kv")
    p = t * K + k
    rows = wq_in.shape[0]
    part = rows // G
    width = wq.shape[0]
    length = normed.shape[0]
    block = length // S
    share = length // TK
    cols = wq.shape[1]
    kcols = kn.shape[1]
    beams = hidden_ref.shape[0]
    steps = ids.shape[0] // beams
    pending = []

    def when(condition, action):
        if condition is True:
            action()
        else:
            pl.when(condition)(action)

    def send(make, condition=True):
        when(condition, lambda: make().start())
        pending.append((make, condition))

    def remote(src, dst, ss, rs, **where):
        return pltpu.make_async_remote_copy(
            src_ref=src, dst_ref=dst, send_sem=ss, recv_sem=rs, device_id=where, device_id_type=MESH
        )

    barrier = pltpu.get_barrier_semaphore()
    for j in range(1, S):
        pl.semaphore_signal(barrier, inc=1, device_id={"seq": lax.rem(s + j, S)}, device_id_type=MESH)
    for j in range(1, G):
        pl.semaphore_signal(barrier, inc=1, device_id={"groups": lax.rem(g + j, G)}, device_id_type=MESH)
    peers = []
    for j in range(1, TK):
        other = lax.rem(p + j, TK)
        peers.append((j - 1, other, lax.div(other, K), lax.rem(other, K)))
        pl.semaphore_signal(
            barrier, inc=1, device_id={"tp": peers[-1][2], "kv": peers[-1][3]}, device_id_type=MESH
        )

    mine = pl.ds(pl.multiple_of(s * rows, rows), rows)
    stay = pl.ds(pl.multiple_of(s * block, block), block)
    local = [
        pltpu.make_async_copy(a, b, local_sem.at[i])
        for i, (a, b) in enumerate(
            [
                (events.at[s], xb.at[p, stay]),
                (wq_in, wq.at[mine]),
                (wkv_in, wkv.at[:, mine]),
                (table_in, table),
                (history.at[:, 0], hist),
                (wo_in, wo.at[mine]),
                (wc_in, wc.at[:, mine]),
                (dq_in, dq),
                (do_in, do),
            ]
        )
    ]
    for copy in local:
        copy.start()
    pl.semaphore_wait(barrier, (S - 1) + (G - 1) + (TK - 1))

    for j in range(1, S):

        def make(j=j):
            to = lax.rem(s + j, S)
            return remote(
                events.at[to], xb.at[p, stay], ev_send.at[j - 1], ev_recv.at[j - 1], seq=to
            )

        send(make)

    def at(array, origin, which):
        where = pl.ds(pl.multiple_of(origin * rows + which * part, part), part)
        return [wq, wo][array == 2].at[where] if array in (0, 2) else [wkv, wc][array == 3].at[:, where]

    def own(array):
        where = pl.ds(pl.multiple_of(g * part, part), part)
        source = [wq_in, wkv_in, wo_in, wc_in][array]
        return source.at[where] if array in (0, 2) else source.at[:, where]

    def hop(array, side, r):
        step = 1 if side == 0 else -1

        def make():
            origin = s - step * r
            src = own(array) if r == 0 else at(array, origin, g)
            return remote(
                src, at(array, origin, g), z_send.at[array, side, r], z_recv.at[array, side, r], seq=s + step
            )

        ok = s + step < S if side == 0 else s + step >= 0
        if r > 0:
            ok = jnp.logical_and(ok, s - r >= 0 if side == 0 else s + r < S)
        send(make, ok)

    def across(array, side, r):
        step = 1 if side == 0 else -1
        ok = s - r >= 0 if side == 0 else s + r < S
        for j in range(1, G):

            def make(j=j):
                piece = at(array, s - step * r, g)
                return remote(
                    piece, piece, y_send.at[array, side, r, j - 1], y_recv.at[array, side, r, j - 1],
                    groups=lax.rem(g + j, G),
                )

            send(make, ok)

    def arrive(array, r):
        for side in (0, 1):
            step = 1 if side == 0 else -1
            ok = s - r >= 0 if side == 0 else s + r < S

            def wait(side=side, step=step):
                piece = at(array, s - step * r, g)
                remote(
                    piece, piece, z_send.at[array, side, r - 1], z_recv.at[array, side, r - 1], seq=s
                ).wait_recv()

            when(ok, wait)
            if r + 1 < S:
                hop(array, side, r)
            across(array, side, r)

    def settle(array):
        for r in range(1, S):
            for side in (0, 1):
                step = 1 if side == 0 else -1
                ok = s - r >= 0 if side == 0 else s + r < S

                def wait(side=side, step=step, r=r):
                    for j in range(1, G):
                        piece = at(array, s - step * r, lax.rem(g - j + G, G))
                        remote(
                            piece, piece, y_send.at[array, side, r, j - 1], y_recv.at[array, side, r, j - 1],
                            groups=g,
                        ).wait_recv()

                when(ok, wait)

    def begin(array):
        hop(array, 0, 0)
        hop(array, 1, 0)

    begin(0)
    begin(1)

    def spread(buffer, base):
        def give(source, slot, **where):
            def make():
                piece = buffer.at[source]
                return remote(piece, piece, ag_send.at[slot], ag_recv.at[slot], **where)

            send(make)

        def take(source, slot):
            piece = buffer.at[source]
            remote(piece, piece, ag_send.at[slot], ag_recv.at[slot], tp=t).wait_recv()

        for i in range(1, T):
            give(p, base + i, tp=lax.rem(t + i, T))
        for j in range(1, K):
            give(p, base + T * j, kv=lax.rem(k + j, K))

        def relay():
            for i in range(1, T):
                there = lax.rem(t - i + T, T) * K + k
                take(there, base + i)
                for j in range(1, K):
                    give(there, base + T * j + i, kv=lax.rem(k + j, K))

        def finish():
            for j in range(1, K):
                for i in range(T):
                    there = lax.rem(t - i + T, T) * K + lax.rem(k - j + K, K)
                    take(there, base + T * j + i)

        return relay, finish

    local[0].wait()
    for j in range(1, S):
        came = pl.ds(pl.multiple_of(lax.rem(s - j + S, S) * block, block), block)
        piece = xb.at[p, came]
        remote(piece, piece, ev_send.at[j - 1], ev_recv.at[j - 1], seq=s).wait_recv()
    relay, finish = spread(xb, 0)

    local[3].wait()
    vocab = table.shape[0]
    onehot = (
        ids[...] == p * vocab + lax.broadcasted_iota(jnp.int32, (ids.shape[0], vocab), 1)
    ).astype(BF16)
    for c in range(TK):
        span = slice(c * cols, (c + 1) * cols)
        look[p, :, span] = dot(onehot, table[:, span]).astype(BF16)

    arrive(0, 1)
    arrive(1, 1)
    relay()
    for slot, other, pt, pk in peers:

        def make(slot=slot, pt=pt, pk=pk):
            return remote(look.at[p], look.at[p], lk_send.at[slot], lk_recv.at[slot], tp=pt, kv=pk)

        send(make)
    finish()
    for c in range(S):
        lines = slice(c * block, (c + 1) * block)
        source = [xb[q, lines].astype(F32) for q in range(TK)]
        square = sum(jnp.sum(v * v, axis=-1, keepdims=True) for v in source)
        scale = lax.rsqrt(square / width + eps)
        for q in range(TK):
            span = slice(q * cols, (q + 1) * cols)
            normed[lines, span] = (source[q] * scale * egain[:, span]).astype(BF16)
    for r in range(2, S):
        arrive(0, r)
        arrive(1, r)
    begin(2)
    begin(3)
    for i in (1, 2, 4):
        local[i].wait()
    settle(0)
    settle(1)

    qs[...] = dot(normed[...], wq[...]).astype(BF16)
    kn[...] = dot(normed[...], wkv[0]).astype(BF16)
    vn[...] = dot(normed[...], wkv[1]).astype(BF16)

    heads = cols // DH
    ratio = cols // kcols
    limit = counts[0] * BLK
    chunk = min(128, length)
    turns = [(a, r) for r in range(1, S) for a in (2, 3)]
    spots = heads * (length // chunk)
    done = 0
    spot = 0
    for h in range(heads):
        hs = slice(h * DH, (h + 1) * DH)
        ks = slice(h // ratio * DH, (h // ratio + 1) * DH)
        for c in range(length // chunk):
            lines = slice(c * chunk, (c + 1) * chunk)
            reach = (c + 1) * chunk
            q = qs[lines, hs]
            old = jnp.exp(dot_t(q, hist[0, :, ks]) * DH ** (-0.5))
            new = jnp.exp(dot_t(q, kn[:reach, ks]) * DH ** (-0.5))
            qi = lax.broadcasted_iota(jnp.int32, (chunk, reach), 0) + c * chunk
            ki = lax.broadcasted_iota(jnp.int32, (chunk, reach), 1)
            new = jnp.where((ki <= qi) & (ki < limit), new, 0.0)
            total = jnp.sum(old, axis=-1, keepdims=True) + jnp.sum(new, axis=-1, keepdims=True)
            att[lines, hs] = (
                dot((old / total).astype(BF16), hist[1, :, ks])
                + dot((new / total).astype(BF16), vn[:reach, ks])
            ).astype(BF16)
            spot += 1
            while done * spots < (spot - spots // 4) * len(turns):
                arrive(*turns[done])
                done += 1
    while done < len(turns):
        arrive(*turns[done])
        done += 1
    local[5].wait()
    settle(2)

    def project(which):
        lines = pl.ds(pl.multiple_of(which * share, share), share)
        for c in range(TK):
            span = slice(c * cols, (c + 1) * cols)
            gterm[which, :, span] = dot_t(att[lines, :], wo[span, :]).astype(BF16)

    for j in range(1, K):
        pk = lax.rem(k + j, K)
        for i in range(T):
            it = lax.rem(t + 1 + i, T)
            project(it * K + pk)

            def make(j=j, i=i, pk=pk, it=it):
                return remote(
                    gterm.at[it * K + pk], rk.at[j - 1, i], rk_send.at[j - 1, i], rk_recv.at[j - 1, i], kv=pk
                )

            send(make)
    for i in range(T):
        project(lax.rem(t + 1 + i, T) * K + k)
    total = None
    for i in range(T):
        for j in range(1, K):
            piece = rk.at[j - 1, i]
            remote(piece, piece, rk_send.at[j - 1, i], rk_recv.at[j - 1, i], kv=k).wait_recv()
        it = lax.rem(t + 1 + i, T)
        total = gterm[it * K + k].astype(F32)
        for j in range(1, K):
            total = total + rk[j - 1, i].astype(F32)
        if i < T - 1:
            s1[i] = total.astype(BF16)

            def make(i=i, it=it):
                return remote(s1.at[i], rt.at[i], rt_send.at[i], rt_recv.at[i], tp=it)

            send(make)
        else:
            mixed_ref[...] = total
    for i in range(T - 1):
        remote(rt.at[i], rt.at[i], rt_send.at[i], rt_recv.at[i], tp=t).wait_recv()
    total = mixed_ref[...]
    for i in range(T - 1):
        total = total + rt[i].astype(F32)
    mine = pl.ds(pl.multiple_of(p * share, share), share)
    mixed_ref[...] = total
    square = jnp.zeros((share, 1), F32)
    for q in range(TK):
        span = slice(q * cols, (q + 1) * cols)
        value = mixed_ref[:, span] + xb[q, mine].astype(F32)
        mixed_ref[:, span] = value
        square = square + jnp.sum(value * value, axis=-1, keepdims=True)
        enc_out[:, span] = value.astype(BF16)
    scale = lax.rsqrt(square / width + eps)
    cx[p] = (mixed_ref[...] * scale * cgain[...]).astype(BF16)
    relay, finish = spread(cx, TK)

    local[7].wait()
    local[8].wait()
    for slot, other, pt, pk in peers:
        piece = look.at[lax.rem(p - slot - 1 + TK, TK)]
        remote(piece, piece, lk_send.at[slot], lk_recv.at[slot], tp=t).wait_recv()

    def code(level):
        lines = slice(level * beams, (level + 1) * beams)
        return sum(look[q, lines].astype(F32) for q in range(TK))

    def query():
        hidden = hidden_ref[...]
        return dot((hidden * unit(hidden) * dgain[...]).astype(BF16), dq[...]).astype(BF16)

    hidden_ref[...] = code(0)
    queries = query()
    relay()
    local[6].wait()
    settle(3)
    finish()
    for q in range(TK):
        lines = slice(q * share, (q + 1) * share)
        ck[lines] = dot(cx[q], wc[0]).astype(BF16)
        cv[lines] = dot(cx[q], wc[1]).astype(BF16)

    live = lax.broadcasted_iota(jnp.int32, (ratio * beams, length), 1) < limit
    for level in range(steps):
        for j in range(kcols // DH):
            ks = slice(j * DH, (j + 1) * DH)
            q = jnp.concatenate(
                [queries[:, (j * ratio + a) * DH : (j * ratio + a + 1) * DH] for a in range(ratio)], axis=0
            )
            raised = jnp.where(live, jnp.exp(dot_t(q, ck[:, ks]) * DH ** (-0.5)), 0.0)
            soft = (raised / jnp.sum(raised, axis=-1, keepdims=True)).astype(BF16)
            found = dot(soft, cv[:, ks]).astype(BF16)
            for a in range(ratio):
                h = j * ratio + a
                ba[:, h * DH : (h + 1) * DH] = found[a * beams : (a + 1) * beams]
        if level < steps - 1:
            for c in range(TK):
                span = slice(c * cols, (c + 1) * cols)
                terms[level, p, :, span] = dot_t(ba[...], do[span, :]).astype(BF16)
            for slot, other, pt, pk in peers:

                def make(slot=slot, pt=pt, pk=pk, level=level):
                    piece = terms.at[level, p]
                    return remote(
                        piece, piece, tm_send.at[level, slot], tm_recv.at[level, slot], tp=pt, kv=pk
                    )

                send(make)
            lines = slice(level * beams, (level + 1) * beams)
            pick = (
                parents[lines, :] == lax.broadcasted_iota(jnp.int32, (beams, beams), 1)
            ).astype(F32)
            nextcode = code(level + 1)
            for slot, other, pt, pk in peers:
                piece = terms.at[level, lax.rem(p - slot - 1 + TK, TK)]
                remote(piece, piece, tm_send.at[level, slot], tm_recv.at[level, slot], tp=t).wait_recv()
            state = hidden_ref[...] + sum(terms[level, q].astype(F32) for q in range(TK))
            moved = jnp.dot(pick, state, preferred_element_type=F32, precision=lax.Precision.HIGHEST)
            hidden_ref[...] = moved + nextcode
            queries = query()
        else:
            for c in range(TK):
                span = slice(c * cols, (c + 1) * cols)
                term = dot_t(ba[...], do[span, :])
                last_own[c] = term.astype(BF16)
            for slot, other, pt, pk in peers:

                def make(slot=slot, other=other, pt=pt, pk=pk, level=level):
                    return remote(
                        last_own.at[other], last_in.at[slot],
                        tm_send.at[level, slot], tm_recv.at[level, slot], tp=pt, kv=pk,
                    )

                send(make)
            value = jnp.zeros((beams, cols), F32)
            for c in range(TK):
                span = slice(c * cols, (c + 1) * cols)
                value = jnp.where(p == c, hidden_ref[:, span], value)
            value = value + last_own[p].astype(F32)
            for slot, other, pt, pk in peers:
                piece = last_in.at[slot]
                remote(piece, piece, tm_send.at[level, slot], tm_recv.at[level, slot], tp=t).wait_recv()
            for slot in range(TK - 1):
                value = value + last_in[slot].astype(F32)
            beam_out[...] = value.astype(BF16)

    for make, condition in pending:
        when(condition, lambda make=make: make().wait_send())


def solution(mesh):
    G, S, T, K = (mesh.shape[a] for a in ("groups", "seq", "tp", "kv"))
    TK = T * K

    def shards(
        events, history, counts, ids, parents, wq, wkv, wo, wc, dq, do, table, egain, cgain, dgain
    ):
        users, block, cols = events.shape
        length = block * S
        share = length // TK
        rows, kcols = wkv.shape[1:]
        width = rows * S
        steps, beams = ids.shape
        hist_len = history.shape[2]
        vm = lambda *shape: pltpu.VMEM(shape, BF16)
        vf = lambda *shape: pltpu.VMEM(shape, F32)
        dma = lambda *shape: pltpu.SemaphoreType.DMA(shape)
        anywhere = pl.BlockSpec(memory_space=pl.ANY)
        vmem = pl.BlockSpec(memory_space=pltpu.VMEM)
        smem = pl.BlockSpec(memory_space=pltpu.SMEM)
        enc, beam = pl.pallas_call(
            functools.partial(body, (G, S, T, K)),
            out_shape=(
                jax.ShapeDtypeStruct((share, width), BF16),
                jax.ShapeDtypeStruct((beams, cols), BF16),
            ),
            in_specs=[anywhere, anywhere, smem, vmem, vmem] + [anywhere] * 7 + [vmem] * 3,
            out_specs=(vmem, vmem),
            scratch_shapes=[
                vm(width, cols), vm(2, width, kcols), vm(width, cols), vm(2, width, kcols),
                vm(width, cols), vm(width, cols), vm(*table.shape), vm(2, hist_len, kcols),
                vm(TK, length, cols), vm(length, width),
                vm(length, cols), vm(length, kcols), vm(length, kcols), vm(length, cols),
                vm(TK, share, width), vm(max(K - 1, 1), T, share, width), vm(max(T - 1, 1), share, width),
                vm(max(T - 1, 1), share, width), vm(TK, share, width), vm(length, kcols), vm(length, kcols),
                vm(TK, steps * beams, width), vm(steps, TK, beams, width),
                vm(TK, beams, cols), vm(TK, beams, cols),
                vf(beams, width), vf(share, width), vm(beams, cols),
                dma(9), dma(4, 2, S), dma(4, 2, S), dma(4, 2, S, G), dma(4, 2, S, G), dma(S), dma(S),
                dma(2 * TK), dma(2 * TK), dma(TK), dma(TK), dma(K, T), dma(K, T), dma(T), dma(T),
                dma(steps, TK), dma(steps, TK),
            ],
            compiler_params=pltpu.CompilerParams(
                collective_id=0, has_side_effects=True, vmem_limit_bytes=60 * 1024 * 1024
            ),
        )(
            events, history, counts, ids.reshape(-1, 1), parents.reshape(-1, 1), wq, wkv, wo, wc, dq, do,
            table, egain[None], cgain[None], dgain[None],
        )
        return enc[None], beam

    in_specs = (
        P("groups", "seq", ("tp", "kv")),
        P(None, ("groups", "seq"), None, ("tp", "kv")),
        P(("groups", "seq")),
        P(None, ("groups", "seq")),
        P(None, ("groups", "seq")),
        P("seq", ("tp", "kv")),
        P(None, "seq", ("tp", "kv")),
        P("seq", ("tp", "kv")),
        P(None, "seq", ("tp", "kv")),
        P(None, ("tp", "kv")),
        P(None, ("tp", "kv")),
        P(("tp", "kv"), None),
        P(),
        P(),
        P(),
    )
    out_specs = (P(("groups", "seq"), ("tp", "kv"), None), P(("groups", "seq"), ("tp", "kv")))
    return jax.shard_map(shards, mesh=mesh, in_specs=in_specs, out_specs=out_specs, check_vma=False)
```

```python
import functools

import jax
import jax.numpy as jnp
from jax import lax
from jax.experimental import pallas as pl
from jax.experimental.pallas import tpu as pltpu
from jax.sharding import PartitionSpec as P

DH = 128
BLK = 128
eps = 1e-06
F32 = jnp.float32
BF16 = jnp.bfloat16
MESH = pl.DeviceIdType.MESH


def unit(values):
    return lax.rsqrt(jnp.mean(values * values, axis=-1, keepdims=True) + eps)


def dot(a, b):
    return jnp.dot(a, b, preferred_element_type=F32)


def dot_t(a, b):
    return lax.dot_general(a, b, (((1,), (1,)), ((), ())), preferred_element_type=F32)


def body(
    sizes,
    events, history, counts, ids, parents, wq_in, wkv_in, wo_in, wc_in, dq_in, do_in, table_in,
    egain, cgain, dgain,
    enc_out, beam_out,
    wq, wkv, wo, wc, dq, do, table, hist, xb, normed, qs, kn, vn, att, gterm, rk, s1, rt, cx, ck, cv,
    look, terms, last_own, last_in, hidden_ref, mixed_ref, ba, old,
    local_sem, z_send, z_recv, y_send, y_recv, ev_send, ev_recv,
    ag_send, ag_recv, lk_send, lk_recv, rk_send, rk_recv, rt_send, rt_recv, tm_send, tm_recv,
):
    G, S, T, K = sizes
    TK = T * K
    g, s = lax.axis_index("groups"), lax.axis_index("seq")
    t, k = lax.axis_index("tp"), lax.axis_index("kv")
    p = t * K + k
    rows = wq_in.shape[0]
    part = rows // G
    width = wq.shape[0]
    length = normed.shape[0]
    block = length // S
    share = length // TK
    cols = wq.shape[1]
    kcols = kn.shape[1]
    beams = hidden_ref.shape[0]
    steps = ids.shape[0]
    pending = []

    def when(condition, action):
        if condition is True:
            action()
        else:
            pl.when(condition)(action)

    def send(make, condition=True):
        when(condition, lambda: make().start())
        pending.append((make, condition))

    def remote(src, dst, ss, rs, **where):
        return pltpu.make_async_remote_copy(
            src_ref=src, dst_ref=dst, send_sem=ss, recv_sem=rs, device_id=where, device_id_type=MESH
        )

    barrier = pltpu.get_barrier_semaphore()
    for j in range(1, S):
        pl.semaphore_signal(barrier, inc=1, device_id={"seq": lax.rem(s + j, S)}, device_id_type=MESH)
    for j in range(1, G):
        pl.semaphore_signal(barrier, inc=1, device_id={"groups": lax.rem(g + j, G)}, device_id_type=MESH)
    peers = []
    for j in range(1, TK):
        other = lax.rem(p + j, TK)
        peers.append((j - 1, other, lax.div(other, K), lax.rem(other, K)))
        pl.semaphore_signal(
            barrier, inc=1, device_id={"tp": peers[-1][2], "kv": peers[-1][3]}, device_id_type=MESH
        )

    mine = pl.ds(pl.multiple_of(s * rows, rows), rows)
    stay = pl.ds(pl.multiple_of(s * block, block), block)
    local = [
        pltpu.make_async_copy(a, b, local_sem.at[i])
        for i, (a, b) in enumerate(
            [
                (events.at[s], xb.at[p, stay]),
                (wq_in, wq.at[mine]),
                (wkv_in, wkv.at[:, mine]),
                (table_in, table),
                (history.at[:, 0], hist),
                (wo_in, wo.at[mine]),
                (wc_in, wc.at[:, mine]),
                (dq_in, dq),
                (do_in, do),
            ]
        )
    ]
    for copy in local:
        copy.start()
    pl.semaphore_wait(barrier, (S - 1) + (G - 1) + (TK - 1))

    for j in range(1, S):

        def make(j=j):
            to = lax.rem(s + j, S)
            return remote(
                events.at[to], xb.at[p, stay], ev_send.at[j - 1], ev_recv.at[j - 1], seq=to
            )

        send(make)

    arrays = [
        (wq, wq_in, None, 0, 2), (wq, wq_in, None, 1, 2),
        (wkv, wkv_in, 0, 0, 1), (wkv, wkv_in, 1, 0, 1),
        (wo, wo_in, None, 0, 2), (wo, wo_in, None, 1, 2),
        (wc, wc_in, slice(None), 0, 1),
    ]

    def cut(ref, array, start):
        lead, sub, of = arrays[array][2:]
        size = part // of
        where = pl.ds(pl.multiple_of(start + sub * size, size), size)
        return ref.at[where] if lead is None else ref.at[lead, where]

    def at(array, origin, which):
        return cut(arrays[array][0], array, origin * rows + which * part)

    def own(array):
        return cut(arrays[array][1], array, g * part)

    def there(side, r):
        return s - r >= 0 if side == 0 else s + r < S

    def hop(array, side, r):
        step = 1 if side == 0 else -1

        def make():
            origin = s - step * r
            src = own(array) if r == 0 else at(array, origin, g)
            return remote(
                src, at(array, origin, g), z_send.at[array, side, r], z_recv.at[array, side, r], seq=s + step
            )

        ok = s + step < S if side == 0 else s + step >= 0
        if r > 0:
            ok = jnp.logical_and(ok, there(side, r))
        send(make, ok)

    def across(array, side, r):
        step = 1 if side == 0 else -1
        for j in range(1, G):

            def make(j=j):
                piece = at(array, s - step * r, g)
                return remote(
                    piece, piece, y_send.at[array, side, r, j - 1], y_recv.at[array, side, r, j - 1],
                    groups=lax.rem(g + j, G),
                )

            send(make, there(side, r))

    def arrive(array, r):
        for side in (0, 1):
            step = 1 if side == 0 else -1

            def wait(side=side, step=step):
                piece = at(array, s - step * r, g)
                remote(
                    piece, piece, z_send.at[array, side, r - 1], z_recv.at[array, side, r - 1], seq=s
                ).wait_recv()

            when(there(side, r), wait)
            if r + 1 < S:
                hop(array, side, r)
            across(array, side, r)

    def settle(array):
        for r in range(1, S):
            for side in (0, 1):
                step = 1 if side == 0 else -1

                def wait(side=side, step=step, r=r):
                    for j in range(1, G):
                        piece = at(array, s - step * r, lax.rem(g - j + G, G))
                        remote(
                            piece, piece, y_send.at[array, side, r, j - 1], y_recv.at[array, side, r, j - 1],
                            groups=g,
                        ).wait_recv()

                when(there(side, r), wait)

    def begin(array):
        hop(array, 0, 0)
        hop(array, 1, 0)

    stages = [(0, 1), (2, 3), (4, 5), (6,)]
    order = [("begin", a, 0) for a in stages[0]]
    for n, stage in enumerate(stages):
        for r in range(1, S):
            order += [("arrive", a, r) for a in stage]
            if r == max(S - 2, 1) and n + 1 < len(stages):
                order += [("begin", a, 0) for a in stages[n + 1]]
    progress = [0]

    def upto(stage, r):
        goal = max(
            i for i, (what, a, level) in enumerate(order)
            if (what == "arrive" and a in stages[stage] and level <= r)
            or (what == "begin" and stage + 1 < len(stages) and a in stages[stage + 1] and r >= max(S - 2, 1))
            or (what == "begin" and a in stages[stage])
        )
        while progress[0] <= goal:
            what, a, level = order[progress[0]]
            if what == "begin":
                begin(a)
            else:
                arrive(a, level)
            progress[0] += 1

    near, far, end = max(S - 3, 1), max(S - 2, 1), S - 1
    upto(0, 0)

    def spread(buffer, base, lines):
        def give(source, slot, **where):
            def make():
                piece = buffer.at[source, lines]
                return remote(piece, piece, ag_send.at[base, slot], ag_recv.at[base, slot], **where)

            send(make)

        def take(source, slot):
            piece = buffer.at[source, lines]
            remote(piece, piece, ag_send.at[base, slot], ag_recv.at[base, slot], tp=t).wait_recv()

        for i in range(1, T):
            give(p, i, tp=lax.rem(t + i, T))
        for j in range(1, K):
            give(p, T * j, kv=lax.rem(k + j, K))

        def relay():
            for i in range(1, T):
                there = lax.rem(t - i + T, T) * K + k
                take(there, i)
                for j in range(1, K):
                    give(there, T * j + i, kv=lax.rem(k + j, K))

        def finish():
            for j in range(1, K):
                for i in range(T):
                    there = lax.rem(t - i + T, T) * K + lax.rem(k - j + K, K)
                    take(there, T * j + i)

        return relay, finish

    moves = []
    for j in range(S):
        came = pl.ds(pl.multiple_of(lax.rem(s - j + S, S) * block, block), block)
        if j == 0:
            local[0].wait()
        else:
            piece = xb.at[p, came]
            remote(piece, piece, ev_send.at[j - 1], ev_recv.at[j - 1], seq=s).wait_recv()
        moves.append(spread(xb, j, came) + (came,))

    local[3].wait()
    vocab = table.shape[0]
    column = jnp.zeros((steps * beams, 1), jnp.int32)
    line = lax.broadcasted_iota(jnp.int32, column.shape, 0)
    for r in range(steps * beams):
        column = jnp.where(line == r, ids[r // beams, r % beams], column)
    onehot = (
        column == p * vocab + lax.broadcasted_iota(jnp.int32, (steps * beams, vocab), 1)
    ).astype(BF16)
    for c in range(TK):
        span = slice(c * cols, (c + 1) * cols)
        look[p, :, span] = dot(onehot, table[:, span]).astype(BF16)

    upto(0, near)
    for relay, finish, came in moves:
        relay()
    for slot, other, pt, pk in peers:

        def make(slot=slot, pt=pt, pk=pk):
            return remote(look.at[p], look.at[p], lk_send.at[slot], lk_recv.at[slot], tp=pt, kv=pk)

        send(make)
    upto(0, far)
    for relay, finish, came in moves:
        finish()
        source = [xb[q, came].astype(F32) for q in range(TK)]
        square = sum(jnp.sum(v * v, axis=-1, keepdims=True) for v in source)
        scale = lax.rsqrt(square / width + eps)
        for q in range(TK):
            span = slice(q * cols, (q + 1) * cols)
            normed[came, span] = (source[q] * scale * egain[:, span]).astype(BF16)
    upto(0, end)
    upto(1, near)
    local[1].wait()
    local[4].wait()
    settle(0)
    settle(1)
    qs[...] = dot(normed[...], wq[...]).astype(BF16)

    heads = cols // DH
    ratio = cols // kcols
    limit = counts[0] * BLK
    chunk = min(share, length)
    upto(1, far)
    for h in range(heads):
        hs = slice(h * DH, (h + 1) * DH)
        ks = slice(h // ratio * DH, (h // ratio + 1) * DH)
        for c in range(length // chunk):
            lines = slice(c * chunk, (c + 1) * chunk)
            old[h, lines] = jnp.exp(dot_t(qs[lines, hs], hist[0, :, ks]) * DH ** (-0.5))
    upto(1, end)
    local[2].wait()
    settle(2)
    kn[...] = dot(normed[...], wkv[0]).astype(BF16)
    upto(2, near)
    settle(3)
    vn[...] = dot(normed[...], wkv[1]).astype(BF16)

    marks = {1: (2, far), max(heads // 2, 1): (2, end)}
    for h in range(heads):
        hs = slice(h * DH, (h + 1) * DH)
        ks = slice(h // ratio * DH, (h // ratio + 1) * DH)
        for c in range(length // chunk):
            lines = slice(c * chunk, (c + 1) * chunk)
            reach = (c + 1) * chunk
            new = jnp.exp(dot_t(qs[lines, hs], kn[:reach, ks]) * DH ** (-0.5))
            qi = lax.broadcasted_iota(jnp.int32, (chunk, reach), 0) + c * chunk
            ki = lax.broadcasted_iota(jnp.int32, (chunk, reach), 1)
            new = jnp.where((ki <= qi) & (ki < limit), new, 0.0)
            past = old[h, lines]
            total = jnp.sum(past, axis=-1, keepdims=True) + jnp.sum(new, axis=-1, keepdims=True)
            att[lines, hs] = (
                dot((past / total).astype(BF16), hist[1, :, ks])
                + dot((new / total).astype(BF16), vn[:reach, ks])
            ).astype(BF16)
        if h + 1 < heads and h + 1 in marks:
            upto(*marks[h + 1])
    upto(2, end)
    upto(3, near)
    local[5].wait()
    settle(4)
    settle(5)

    def lines_of(which):
        return pl.ds(pl.multiple_of(which * share, share), share)

    def pass_on(c):
        span = slice(c * cols, (c + 1) * cols)
        for i in range(T):
            it = lax.rem(t + 1 + i, T)
            for j in range(1, K):
                piece = rk.at[c, j - 1, i]
                remote(piece, piece, rk_send.at[c, j - 1, i], rk_recv.at[c, j - 1, i], kv=k).wait_recv()
            total = gterm[c, lines_of(it * K + k)].astype(F32)
            for j in range(1, K):
                total = total + rk[c, j - 1, i].astype(F32)
            if i < T - 1:
                s1[c, i] = total.astype(BF16)

                def make(i=i, it=it):
                    return remote(s1.at[c, i], rt.at[c, i], rt_send.at[c, i], rt_recv.at[c, i], tp=it)

                send(make)
            else:
                mixed_ref[:, span] = total

    for c in range(TK):
        gterm[c] = dot_t(att[...], wo[c * cols : (c + 1) * cols, :]).astype(BF16)
        for j in range(1, K):
            pk = lax.rem(k + j, K)
            for i in range(T):

                def make(c=c, j=j, i=i, pk=pk):
                    return remote(
                        gterm.at[c, lines_of(lax.rem(t + 1 + i, T) * K + pk)], rk.at[c, j - 1, i],
                        rk_send.at[c, j - 1, i], rk_recv.at[c, j - 1, i], kv=pk,
                    )

                send(make)
        if c > 0:
            pass_on(c - 1)
    pass_on(TK - 1)
    upto(3, far)
    square = jnp.zeros((share, 1), F32)
    mine = lines_of(p)
    for q in range(TK):
        for i in range(T - 1):
            remote(rt.at[q, i], rt.at[q, i], rt_send.at[q, i], rt_recv.at[q, i], tp=t).wait_recv()
        span = slice(q * cols, (q + 1) * cols)
        value = mixed_ref[:, span]
        for i in range(T - 1):
            value = value + rt[q, i].astype(F32)
        value = value + xb[q, mine].astype(F32)
        mixed_ref[:, span] = value
        square = square + jnp.sum(value * value, axis=-1, keepdims=True)
        enc_out[:, span] = value.astype(BF16)
    scale = lax.rsqrt(square / width + eps)
    cx[p] = (mixed_ref[...] * scale * cgain[...]).astype(BF16)
    relay, finish = spread(cx, S, pl.ds(0, share))
    upto(3, end)

    local[7].wait()
    local[8].wait()
    for slot, other, pt, pk in peers:
        piece = look.at[lax.rem(p - slot - 1 + TK, TK)]
        remote(piece, piece, lk_send.at[slot], lk_recv.at[slot], tp=t).wait_recv()

    def code(level):
        lines = slice(level * beams, (level + 1) * beams)
        return sum(look[q, lines].astype(F32) for q in range(TK))

    def query():
        hidden = hidden_ref[...]
        return dot((hidden * unit(hidden) * dgain[...]).astype(BF16), dq[...]).astype(BF16)

    hidden_ref[...] = code(0)
    queries = query()
    relay()
    local[6].wait()
    settle(6)
    finish()
    across_in = cx[...].reshape(length, width)
    ck[...] = dot(across_in, wc[0]).astype(BF16)
    cv[...] = dot(across_in, wc[1]).astype(BF16)

    live = lax.broadcasted_iota(jnp.int32, (ratio * beams, length), 1) < limit
    for level in range(steps):
        for j in range(kcols // DH):
            ks = slice(j * DH, (j + 1) * DH)
            q = jnp.concatenate(
                [queries[:, (j * ratio + a) * DH : (j * ratio + a + 1) * DH] for a in range(ratio)], axis=0
            )
            raised = jnp.where(live, jnp.exp(dot_t(q, ck[:, ks]) * DH ** (-0.5)), 0.0)
            soft = (raised / jnp.sum(raised, axis=-1, keepdims=True)).astype(BF16)
            found = dot(soft, cv[:, ks]).astype(BF16)
            for a in range(ratio):
                h = j * ratio + a
                ba[:, h * DH : (h + 1) * DH] = found[a * beams : (a + 1) * beams]
        if level < steps - 1:
            for c in range(TK):
                span = slice(c * cols, (c + 1) * cols)
                terms[level, p, :, span] = dot_t(ba[...], do[span, :]).astype(BF16)
            for slot, other, pt, pk in peers:

                def make(slot=slot, pt=pt, pk=pk, level=level):
                    piece = terms.at[level, p]
                    return remote(
                        piece, piece, tm_send.at[level, slot], tm_recv.at[level, slot], tp=pt, kv=pk
                    )

                send(make)
            column = jnp.zeros((beams, 1), jnp.int32)
            line = lax.broadcasted_iota(jnp.int32, column.shape, 0)
            for r in range(beams):
                column = jnp.where(line == r, parents[level, r], column)
            pick = (
                column == lax.broadcasted_iota(jnp.int32, (beams, beams), 1)
            ).astype(F32)
            nextcode = code(level + 1)
            for slot, other, pt, pk in peers:
                piece = terms.at[level, lax.rem(p - slot - 1 + TK, TK)]
                remote(piece, piece, tm_send.at[level, slot], tm_recv.at[level, slot], tp=t).wait_recv()
            state = hidden_ref[...] + sum(terms[level, q].astype(F32) for q in range(TK))
            moved = jnp.dot(pick, state, preferred_element_type=F32, precision=lax.Precision.HIGHEST)
            hidden_ref[...] = moved + nextcode
            queries = query()
        else:
            for c in range(TK):
                span = slice(c * cols, (c + 1) * cols)
                term = dot_t(ba[...], do[span, :])
                last_own[c] = term.astype(BF16)
            for slot, other, pt, pk in peers:

                def make(slot=slot, other=other, pt=pt, pk=pk, level=level):
                    return remote(
                        last_own.at[other], last_in.at[slot],
                        tm_send.at[level, slot], tm_recv.at[level, slot], tp=pt, kv=pk,
                    )

                send(make)
            value = jnp.zeros((beams, cols), F32)
            for c in range(TK):
                span = slice(c * cols, (c + 1) * cols)
                value = jnp.where(p == c, hidden_ref[:, span], value)
            value = value + last_own[p].astype(F32)
            for slot, other, pt, pk in peers:
                piece = last_in.at[slot]
                remote(piece, piece, tm_send.at[level, slot], tm_recv.at[level, slot], tp=t).wait_recv()
            for slot in range(TK - 1):
                value = value + last_in[slot].astype(F32)
            beam_out[...] = value.astype(BF16)

    for make, condition in pending:
        when(condition, lambda make=make: make().wait_send())


def solution(mesh):
    G, S, T, K = (mesh.shape[a] for a in ("groups", "seq", "tp", "kv"))
    TK = T * K

    def shards(
        events, history, counts, ids, parents, wq, wkv, wo, wc, dq, do, table, egain, cgain, dgain
    ):
        users, block, cols = events.shape
        length = block * S
        share = length // TK
        rows, kcols = wkv.shape[1:]
        width = rows * S
        steps, beams = ids.shape
        hist_len = history.shape[2]
        vm = lambda *shape: pltpu.VMEM(shape, BF16)
        vf = lambda *shape: pltpu.VMEM(shape, F32)
        dma = lambda *shape: pltpu.SemaphoreType.DMA(shape)
        anywhere = pl.BlockSpec(memory_space=pl.ANY)
        vmem = pl.BlockSpec(memory_space=pltpu.VMEM)
        smem = pl.BlockSpec(memory_space=pltpu.SMEM)
        enc, beam = pl.pallas_call(
            functools.partial(body, (G, S, T, K)),
            out_shape=(
                jax.ShapeDtypeStruct((share, width), BF16),
                jax.ShapeDtypeStruct((beams, cols), BF16),
            ),
            in_specs=[anywhere, anywhere, smem, smem, smem] + [anywhere] * 7 + [vmem] * 3,
            out_specs=(vmem, vmem),
            scratch_shapes=[
                vm(width, cols), vm(2, width, kcols), vm(width, cols), vm(2, width, kcols),
                vm(width, cols), vm(width, cols), vm(*table.shape), vm(2, hist_len, kcols),
                vm(TK, length, cols), vm(length, width),
                vm(length, cols), vm(length, kcols), vm(length, kcols), vm(length, cols),
                vm(TK, length, cols), vm(TK, max(K - 1, 1), T, share, cols), vm(TK, max(T - 1, 1), share, cols),
                vm(TK, max(T - 1, 1), share, cols), vm(TK, share, width), vm(length, kcols), vm(length, kcols),
                vm(TK, steps * beams, width), vm(steps, TK, beams, width),
                vm(TK, beams, cols), vm(TK, beams, cols),
                vf(beams, width), vf(share, width), vm(beams, cols),
                vf(cols // DH, length, hist_len),
                dma(9), dma(7, 2, S), dma(7, 2, S), dma(7, 2, S, G), dma(7, 2, S, G), dma(S), dma(S),
                dma(S + 1, TK), dma(S + 1, TK), dma(TK), dma(TK), dma(TK, K, T), dma(TK, K, T), dma(TK, T),
                dma(TK, T),
                dma(steps, TK), dma(steps, TK),
            ],
            compiler_params=pltpu.CompilerParams(
                collective_id=0, has_side_effects=True, vmem_limit_bytes=60 * 1024 * 1024
            ),
        )(
            events, history, counts, ids, parents, wq, wkv, wo, wc, dq, do,
            table, egain[None], cgain[None], dgain[None],
        )
        return enc[None], beam

    in_specs = (
        P("groups", "seq", ("tp", "kv")),
        P(None, ("groups", "seq"), None, ("tp", "kv")),
        P(("groups", "seq")),
        P(None, ("groups", "seq")),
        P(None, ("groups", "seq")),
        P("seq", ("tp", "kv")),
        P(None, "seq", ("tp", "kv")),
        P("seq", ("tp", "kv")),
        P(None, "seq", ("tp", "kv")),
        P(None, ("tp", "kv")),
        P(None, ("tp", "kv")),
        P(("tp", "kv"), None),
        P(),
        P(),
        P(),
    )
    out_specs = (P(("groups", "seq"), ("tp", "kv"), None), P(("groups", "seq"), ("tp", "kv")))
    return jax.shard_map(shards, mesh=mesh, in_specs=in_specs, out_specs=out_specs, check_vma=False)
```

```python
import functools

import jax
import jax.numpy as jnp
from jax import lax
from jax.experimental import pallas as pl
from jax.experimental.pallas import tpu as pltpu
from jax.sharding import PartitionSpec as P

DH = 128
BLK = 128
eps = 1e-06
F32 = jnp.float32
BF16 = jnp.bfloat16
MESH = pl.DeviceIdType.MESH


def unit(values):
    return lax.rsqrt(jnp.mean(values * values, axis=-1, keepdims=True) + eps)


def dot(a, b):
    return jnp.dot(a, b, preferred_element_type=F32)


def dot_t(a, b):
    return lax.dot_general(a, b, (((1,), (1,)), ((), ())), preferred_element_type=F32)


def body(
    sizes,
    events, history, counts, ids, parents, wq_in, wkv_in, wo_in, wc_in, dq_in, do_in, table_in,
    egain, cgain, dgain,
    enc_out, beam_out,
    wq, wkv, wo, wc, dq, do, table, hist, xb, normed, qs, kn, vn, att, gterm, rk, s1, rt, cx, ck, cv,
    look, terms, last_own, last_in, hidden_ref, mixed_ref, ba, old,
    local_sem, z_send, z_recv, y_send, y_recv, ev_send, ev_recv,
    ag_send, ag_recv, lk_send, lk_recv, rk_send, rk_recv, rt_send, rt_recv, tm_send, tm_recv,
):
    G, S, T, K = sizes
    TK = T * K
    g, s = lax.axis_index("groups"), lax.axis_index("seq")
    t, k = lax.axis_index("tp"), lax.axis_index("kv")
    p = t * K + k
    rows = wq_in.shape[0]
    part = rows // G
    width = wq.shape[0]
    length = normed.shape[0]
    block = length // S
    share = length // TK
    cols = wq.shape[1]
    kcols = kn.shape[1]
    beams = hidden_ref.shape[0]
    steps = ids.shape[0]
    pending = []

    def when(condition, action):
        if condition is True:
            action()
        else:
            pl.when(condition)(action)

    def send(make, condition=True):
        when(condition, lambda: make().start())
        pending.append((make, condition))

    def remote(src, dst, ss, rs, **where):
        return pltpu.make_async_remote_copy(
            src_ref=src, dst_ref=dst, send_sem=ss, recv_sem=rs, device_id=where, device_id_type=MESH
        )

    barrier = pltpu.get_barrier_semaphore()
    for j in range(1, S):
        pl.semaphore_signal(barrier, inc=1, device_id={"seq": lax.rem(s + j, S)}, device_id_type=MESH)
    for j in range(1, G):
        pl.semaphore_signal(barrier, inc=1, device_id={"groups": lax.rem(g + j, G)}, device_id_type=MESH)
    peers = []
    for j in range(1, TK):
        other = lax.rem(p + j, TK)
        peers.append((j - 1, other, lax.div(other, K), lax.rem(other, K)))
        pl.semaphore_signal(
            barrier, inc=1, device_id={"tp": peers[-1][2], "kv": peers[-1][3]}, device_id_type=MESH
        )

    mine = pl.ds(pl.multiple_of(s * rows, rows), rows)
    stay = pl.ds(pl.multiple_of(s * block, block), block)
    local = [
        pltpu.make_async_copy(a, b, local_sem.at[i])
        for i, (a, b) in enumerate(
            [
                (events.at[s], xb.at[p, stay]),
                (wq_in, wq.at[mine]),
                (wkv_in, wkv.at[:, mine]),
                (table_in, table),
                (history.at[:, 0], hist),
                (wo_in, wo.at[mine]),
                (wc_in, wc.at[:, mine]),
                (dq_in, dq),
                (do_in, do),
            ]
        )
    ]
    for copy in local:
        copy.start()
    pl.semaphore_wait(barrier, (S - 1) + (G - 1) + (TK - 1))

    for j in range(1, S):

        def make(j=j):
            to = lax.rem(s + j, S)
            return remote(
                events.at[to], xb.at[p, stay], ev_send.at[j - 1], ev_recv.at[j - 1], seq=to
            )

        send(make)

    arrays = [
        (wq, wq_in, None, 0, 2), (wq, wq_in, None, 1, 2),
        (wkv, wkv_in, 0, 0, 1), (wkv, wkv_in, 1, 0, 1),
        (wo, wo_in, None, 0, 2), (wo, wo_in, None, 1, 2),
        (wc, wc_in, slice(None), 0, 1),
    ]

    def cut(ref, array, start):
        lead, sub, of = arrays[array][2:]
        size = part // of
        where = pl.ds(pl.multiple_of(start + sub * size, size), size)
        return ref.at[where] if lead is None else ref.at[lead, where]

    def at(array, origin, which):
        return cut(arrays[array][0], array, origin * rows + which * part)

    def own(array):
        return cut(arrays[array][1], array, g * part)

    def there(side, r):
        return s - r >= 0 if side == 0 else s + r < S

    def hop(array, side, r):
        step = 1 if side == 0 else -1

        def make():
            origin = s - step * r
            src = own(array) if r == 0 else at(array, origin, g)
            return remote(
                src, at(array, origin, g), z_send.at[array, side, r], z_recv.at[array, side, r], seq=s + step
            )

        ok = s + step < S if side == 0 else s + step >= 0
        if r > 0:
            ok = jnp.logical_and(ok, there(side, r))
        send(make, ok)

    def across(array, side, r):
        step = 1 if side == 0 else -1
        for j in range(1, G):

            def make(j=j):
                piece = at(array, s - step * r, g)
                return remote(
                    piece, piece, y_send.at[array, side, r, j - 1], y_recv.at[array, side, r, j - 1],
                    groups=lax.rem(g + j, G),
                )

            send(make, there(side, r))

    def arrive(array, r):
        for side in (0, 1):
            step = 1 if side == 0 else -1

            def wait(side=side, step=step):
                piece = at(array, s - step * r, g)
                remote(
                    piece, piece, z_send.at[array, side, r - 1], z_recv.at[array, side, r - 1], seq=s
                ).wait_recv()

            when(there(side, r), wait)
            if r + 1 < S:
                hop(array, side, r)
            across(array, side, r)

    def settle(array):
        for r in range(1, S):
            for side in (0, 1):
                step = 1 if side == 0 else -1

                def wait(side=side, step=step, r=r):
                    for j in range(1, G):
                        piece = at(array, s - step * r, lax.rem(g - j + G, G))
                        remote(
                            piece, piece, y_send.at[array, side, r, j - 1], y_recv.at[array, side, r, j - 1],
                            groups=g,
                        ).wait_recv()

                when(there(side, r), wait)

    def begin(array):
        hop(array, 0, 0)
        hop(array, 1, 0)

    stages = [(0, 1), (2, 3), (4, 5), (6,)]
    order = [("begin", a, 0) for a in stages[0]]
    for n, stage in enumerate(stages):
        for r in range(1, S):
            order += [("arrive", a, r) for a in stage]
            if r == max(S - 2, 1) and 0 < n < len(stages) - 1:
                order += [("begin", a, 0) for a in stages[n + 1]]
    progress = [0]

    def upto(stage, r):
        goal = max(
            i for i, (what, a, level) in enumerate(order)
            if (what == "arrive" and a in stages[stage] and level <= r)
            or (what == "begin" and stage + 1 < len(stages) and a in stages[stage + 1] and r >= max(S - 2, 1))
            or (what == "begin" and a in stages[stage])
        )
        while progress[0] <= goal:
            what, a, level = order[progress[0]]
            if what == "begin":
                begin(a)
            else:
                arrive(a, level)
            progress[0] += 1

    near, far, end = max(S - 3, 1), max(S - 2, 1), S - 1
    upto(0, 0)
    for a in stages[1]:
        begin(a)

    def spread(buffer, base, lines):
        def give(source, slot, **where):
            def make():
                piece = buffer.at[source, lines]
                return remote(piece, piece, ag_send.at[base, slot], ag_recv.at[base, slot], **where)

            send(make)

        def take(source, slot):
            piece = buffer.at[source, lines]
            remote(piece, piece, ag_send.at[base, slot], ag_recv.at[base, slot], tp=t).wait_recv()

        for i in range(1, T):
            give(p, i, tp=lax.rem(t + i, T))
        for j in range(1, K):
            give(p, T * j, kv=lax.rem(k + j, K))

        def relay():
            for i in range(1, T):
                there = lax.rem(t - i + T, T) * K + k
                take(there, i)
                for j in range(1, K):
                    give(there, T * j + i, kv=lax.rem(k + j, K))

        def finish():
            for j in range(1, K):
                for i in range(T):
                    there = lax.rem(t - i + T, T) * K + lax.rem(k - j + K, K)
                    take(there, T * j + i)

        return relay, finish

    moves = []
    for j in range(S):
        came = pl.ds(pl.multiple_of(lax.rem(s - j + S, S) * block, block), block)
        if j == 0:
            local[0].wait()
        else:
            piece = xb.at[p, came]
            remote(piece, piece, ev_send.at[j - 1], ev_recv.at[j - 1], seq=s).wait_recv()
        moves.append(spread(xb, j, came) + (came,))

    upto(0, near)
    local[3].wait()
    vocab = table.shape[0]
    column = jnp.zeros((steps * beams, 1), jnp.int32)
    line = lax.broadcasted_iota(jnp.int32, column.shape, 0)
    for r in range(steps * beams):
        column = jnp.where(line == r, ids[r // beams, r % beams], column)
    onehot = (
        column == p * vocab + lax.broadcasted_iota(jnp.int32, (steps * beams, vocab), 1)
    ).astype(BF16)
    for c in range(TK):
        span = slice(c * cols, (c + 1) * cols)
        look[p, :, span] = dot(onehot, table[:, span]).astype(BF16)

    for relay, finish, came in moves:
        relay()
    for slot, other, pt, pk in peers:

        def make(slot=slot, pt=pt, pk=pk):
            return remote(look.at[p], look.at[p], lk_send.at[slot], lk_recv.at[slot], tp=pt, kv=pk)

        send(make)
    upto(0, far)
    for relay, finish, came in moves:
        finish()
        source = [xb[q, came].astype(F32) for q in range(TK)]
        square = sum(jnp.sum(v * v, axis=-1, keepdims=True) for v in source)
        scale = lax.rsqrt(square / width + eps)
        for q in range(TK):
            span = slice(q * cols, (q + 1) * cols)
            normed[came, span] = (source[q] * scale * egain[:, span]).astype(BF16)
    upto(0, end)
    upto(1, near)
    local[1].wait()
    local[4].wait()
    settle(0)
    settle(1)
    qs[...] = dot(normed[...], wq[...]).astype(BF16)

    heads = cols // DH
    ratio = cols // kcols
    limit = counts[0] * BLK
    chunk = min(share, length)
    upto(1, far)
    for h in range(heads):
        hs = slice(h * DH, (h + 1) * DH)
        ks = slice(h // ratio * DH, (h // ratio + 1) * DH)
        for c in range(length // chunk):
            lines = slice(c * chunk, (c + 1) * chunk)
            old[h, lines] = jnp.exp(dot_t(qs[lines, hs], hist[0, :, ks]) * DH ** (-0.5))
    upto(1, end)
    local[2].wait()
    settle(2)
    kn[...] = dot(normed[...], wkv[0]).astype(BF16)
    upto(2, near)
    settle(3)
    vn[...] = dot(normed[...], wkv[1]).astype(BF16)

    marks = {1: (2, far), max(heads // 2, 1): (2, end)}
    for h in range(heads):
        hs = slice(h * DH, (h + 1) * DH)
        ks = slice(h // ratio * DH, (h // ratio + 1) * DH)
        for c in range(length // chunk):
            lines = slice(c * chunk, (c + 1) * chunk)
            reach = (c + 1) * chunk
            new = jnp.exp(dot_t(qs[lines, hs], kn[:reach, ks]) * DH ** (-0.5))
            qi = lax.broadcasted_iota(jnp.int32, (chunk, reach), 0) + c * chunk
            ki = lax.broadcasted_iota(jnp.int32, (chunk, reach), 1)
            new = jnp.where((ki <= qi) & (ki < limit), new, 0.0)
            past = old[h, lines]
            total = jnp.sum(past, axis=-1, keepdims=True) + jnp.sum(new, axis=-1, keepdims=True)
            att[lines, hs] = (
                dot((past / total).astype(BF16), hist[1, :, ks])
                + dot((new / total).astype(BF16), vn[:reach, ks])
            ).astype(BF16)
        if h + 1 < heads and h + 1 in marks:
            upto(*marks[h + 1])
    upto(2, end)
    upto(3, near)
    local[5].wait()
    settle(4)
    settle(5)

    def lines_of(which):
        return pl.ds(pl.multiple_of(which * share, share), share)

    def pass_on(c):
        span = slice(c * cols, (c + 1) * cols)
        for i in range(T):
            it = lax.rem(t + 1 + i, T)
            for j in range(1, K):
                piece = rk.at[c, j - 1, i]
                remote(piece, piece, rk_send.at[c, j - 1, i], rk_recv.at[c, j - 1, i], kv=k).wait_recv()
            total = gterm[c, lines_of(it * K + k)].astype(F32)
            for j in range(1, K):
                total = total + rk[c, j - 1, i].astype(F32)
            if i < T - 1:
                s1[c, i] = total.astype(BF16)

                def make(i=i, it=it):
                    return remote(s1.at[c, i], rt.at[c, i], rt_send.at[c, i], rt_recv.at[c, i], tp=it)

                send(make)
            else:
                mixed_ref[:, span] = total

    for c in range(TK):
        gterm[c] = dot_t(att[...], wo[c * cols : (c + 1) * cols, :]).astype(BF16)
        for j in range(1, K):
            pk = lax.rem(k + j, K)
            for i in range(T):

                def make(c=c, j=j, i=i, pk=pk):
                    return remote(
                        gterm.at[c, lines_of(lax.rem(t + 1 + i, T) * K + pk)], rk.at[c, j - 1, i],
                        rk_send.at[c, j - 1, i], rk_recv.at[c, j - 1, i], kv=pk,
                    )

                send(make)
        if c > 0:
            pass_on(c - 1)
    pass_on(TK - 1)
    upto(3, far)
    square = jnp.zeros((share, 1), F32)
    mine = lines_of(p)
    for q in range(TK):
        for i in range(T - 1):
            remote(rt.at[q, i], rt.at[q, i], rt_send.at[q, i], rt_recv.at[q, i], tp=t).wait_recv()
        span = slice(q * cols, (q + 1) * cols)
        value = mixed_ref[:, span]
        for i in range(T - 1):
            value = value + rt[q, i].astype(F32)
        value = value + xb[q, mine].astype(F32)
        mixed_ref[:, span] = value
        square = square + jnp.sum(value * value, axis=-1, keepdims=True)
        enc_out[:, span] = value.astype(BF16)
    scale = lax.rsqrt(square / width + eps)
    cx[p] = (mixed_ref[...] * scale * cgain[...]).astype(BF16)
    relay, finish = spread(cx, S, pl.ds(0, share))
    upto(3, end)

    local[7].wait()
    local[8].wait()
    for slot, other, pt, pk in peers:
        piece = look.at[lax.rem(p - slot - 1 + TK, TK)]
        remote(piece, piece, lk_send.at[slot], lk_recv.at[slot], tp=t).wait_recv()

    def code(level):
        lines = slice(level * beams, (level + 1) * beams)
        return sum(look[q, lines].astype(F32) for q in range(TK))

    def query():
        hidden = hidden_ref[...]
        return dot((hidden * unit(hidden) * dgain[...]).astype(BF16), dq[...]).astype(BF16)

    hidden_ref[...] = code(0)
    queries = query()
    relay()
    local[6].wait()
    settle(6)
    finish()
    across_in = cx[...].reshape(length, width)
    ck[...] = dot(across_in, wc[0]).astype(BF16)
    cv[...] = dot(across_in, wc[1]).astype(BF16)

    live = lax.broadcasted_iota(jnp.int32, (ratio * beams, length), 1) < limit
    for level in range(steps):
        for j in range(kcols // DH):
            ks = slice(j * DH, (j + 1) * DH)
            q = jnp.concatenate(
                [queries[:, (j * ratio + a) * DH : (j * ratio + a + 1) * DH] for a in range(ratio)], axis=0
            )
            raised = jnp.where(live, jnp.exp(dot_t(q, ck[:, ks]) * DH ** (-0.5)), 0.0)
            soft = (raised / jnp.sum(raised, axis=-1, keepdims=True)).astype(BF16)
            found = dot(soft, cv[:, ks]).astype(BF16)
            for a in range(ratio):
                h = j * ratio + a
                ba[:, h * DH : (h + 1) * DH] = found[a * beams : (a + 1) * beams]
        if level < steps - 1:
            for c in range(TK):
                span = slice(c * cols, (c + 1) * cols)
                terms[level, p, :, span] = dot_t(ba[...], do[span, :]).astype(BF16)
            for slot, other, pt, pk in peers:

                def make(slot=slot, pt=pt, pk=pk, level=level):
                    piece = terms.at[level, p]
                    return remote(
                        piece, piece, tm_send.at[level, slot], tm_recv.at[level, slot], tp=pt, kv=pk
                    )

                send(make)
            column = jnp.zeros((beams, 1), jnp.int32)
            line = lax.broadcasted_iota(jnp.int32, column.shape, 0)
            for r in range(beams):
                column = jnp.where(line == r, parents[level, r], column)
            pick = (
                column == lax.broadcasted_iota(jnp.int32, (beams, beams), 1)
            ).astype(F32)
            nextcode = code(level + 1)
            for slot, other, pt, pk in peers:
                piece = terms.at[level, lax.rem(p - slot - 1 + TK, TK)]
                remote(piece, piece, tm_send.at[level, slot], tm_recv.at[level, slot], tp=t).wait_recv()
            state = hidden_ref[...] + sum(terms[level, q].astype(F32) for q in range(TK))
            moved = jnp.dot(pick, state, preferred_element_type=F32, precision=lax.Precision.HIGHEST)
            hidden_ref[...] = moved + nextcode
            queries = query()
        else:
            for c in range(TK):
                span = slice(c * cols, (c + 1) * cols)
                term = dot_t(ba[...], do[span, :])
                last_own[c] = term.astype(BF16)
            for slot, other, pt, pk in peers:

                def make(slot=slot, other=other, pt=pt, pk=pk, level=level):
                    return remote(
                        last_own.at[other], last_in.at[slot],
                        tm_send.at[level, slot], tm_recv.at[level, slot], tp=pt, kv=pk,
                    )

                send(make)
            value = jnp.zeros((beams, cols), F32)
            for c in range(TK):
                span = slice(c * cols, (c + 1) * cols)
                value = jnp.where(p == c, hidden_ref[:, span], value)
            value = value + last_own[p].astype(F32)
            for slot, other, pt, pk in peers:
                piece = last_in.at[slot]
                remote(piece, piece, tm_send.at[level, slot], tm_recv.at[level, slot], tp=t).wait_recv()
            for slot in range(TK - 1):
                value = value + last_in[slot].astype(F32)
            beam_out[...] = value.astype(BF16)

    for make, condition in pending:
        when(condition, lambda make=make: make().wait_send())


def solution(mesh):
    G, S, T, K = (mesh.shape[a] for a in ("groups", "seq", "tp", "kv"))
    TK = T * K

    def shards(
        events, history, counts, ids, parents, wq, wkv, wo, wc, dq, do, table, egain, cgain, dgain
    ):
        users, block, cols = events.shape
        length = block * S
        share = length // TK
        rows, kcols = wkv.shape[1:]
        width = rows * S
        steps, beams = ids.shape
        hist_len = history.shape[2]
        vm = lambda *shape: pltpu.VMEM(shape, BF16)
        vf = lambda *shape: pltpu.VMEM(shape, F32)
        dma = lambda *shape: pltpu.SemaphoreType.DMA(shape)
        anywhere = pl.BlockSpec(memory_space=pl.ANY)
        vmem = pl.BlockSpec(memory_space=pltpu.VMEM)
        smem = pl.BlockSpec(memory_space=pltpu.SMEM)
        enc, beam = pl.pallas_call(
            functools.partial(body, (G, S, T, K)),
            out_shape=(
                jax.ShapeDtypeStruct((share, width), BF16),
                jax.ShapeDtypeStruct((beams, cols), BF16),
            ),
            in_specs=[anywhere, anywhere, smem, smem, smem] + [anywhere] * 7 + [vmem] * 3,
            out_specs=(vmem, vmem),
            scratch_shapes=[
                vm(width, cols), vm(2, width, kcols), vm(width, cols), vm(2, width, kcols),
                vm(width, cols), vm(width, cols), vm(*table.shape), vm(2, hist_len, kcols),
                vm(TK, length, cols), vm(length, width),
                vm(length, cols), vm(length, kcols), vm(length, kcols), vm(length, cols),
                vm(TK, length, cols), vm(TK, max(K - 1, 1), T, share, cols), vm(TK, max(T - 1, 1), share, cols),
                vm(TK, max(T - 1, 1), share, cols), vm(TK, share, width), vm(length, kcols), vm(length, kcols),
                vm(TK, steps * beams, width), vm(steps, TK, beams, width),
                vm(TK, beams, cols), vm(TK, beams, cols),
                vf(beams, width), vf(share, width), vm(beams, cols),
                vf(cols // DH, length, hist_len),
                dma(9), dma(7, 2, S), dma(7, 2, S), dma(7, 2, S, G), dma(7, 2, S, G), dma(S), dma(S),
                dma(S + 1, TK), dma(S + 1, TK), dma(TK), dma(TK), dma(TK, K, T), dma(TK, K, T), dma(TK, T),
                dma(TK, T),
                dma(steps, TK), dma(steps, TK),
            ],
            compiler_params=pltpu.CompilerParams(
                collective_id=0, has_side_effects=True, vmem_limit_bytes=60 * 1024 * 1024
            ),
        )(
            events, history, counts, ids, parents, wq, wkv, wo, wc, dq, do,
            table, egain[None], cgain[None], dgain[None],
        )
        return enc[None], beam

    in_specs = (
        P("groups", "seq", ("tp", "kv")),
        P(None, ("groups", "seq"), None, ("tp", "kv")),
        P(("groups", "seq")),
        P(None, ("groups", "seq")),
        P(None, ("groups", "seq")),
        P("seq", ("tp", "kv")),
        P(None, "seq", ("tp", "kv")),
        P("seq", ("tp", "kv")),
        P(None, "seq", ("tp", "kv")),
        P(None, ("tp", "kv")),
        P(None, ("tp", "kv")),
        P(("tp", "kv"), None),
        P(),
        P(),
        P(),
    )
    out_specs = (P(("groups", "seq"), ("tp", "kv"), None), P(("groups", "seq"), ("tp", "kv")))
    return jax.shard_map(shards, mesh=mesh, in_specs=in_specs, out_specs=out_specs, check_vma=False)
```
